32 devices in a mesh: groups: 2 (over y), page: 8 (over z, core), head: 2 (over x), sub: 1.
Axes of the slice: x: 2, y: 2, z: 4, core: 2. Of those that a mesh axis runs over, the one named last changes fastest.
Arguments:
- queries: bfloat16 [128, 3, 16384], P(('groups', 'page', 'sub'), None, 'head'), parts along dimension 0, may hold values from -400 to 400
- page_keys: bfloat16 [128, 128, 1024], P(('groups', 'page'), None, 'head'), parts along dimension 0, may hold values from -6 to 6
- page_values: bfloat16 [128, 128, 1024], P(('groups', 'page'), None, 'head'), parts along dimension 0, may hold values from -6 to 6
- page_count: int32 [128], P(('groups', 'page')), parts along dimension 0, may hold values from 1 to 128
- leaf_keys: bfloat16 [128, 128, 1024], P(('groups', 'page', 'sub'), None, 'head'), parts along dimension 0, may hold values from -6 to 6
- leaf_values: bfloat16 [128, 128, 1024], P(('groups', 'page', 'sub'), None, 'head'), parts along dimension 0, may hold values from -6 to 6
- leaf_count: int32 [128], P(('groups', 'page', 'sub')), parts along dimension 0, may hold values from 1 to 128
- new_keys: bfloat16 [128, 3, 1024], P(('groups', 'page', 'sub'), None, 'head'), parts along dimension 0, may hold values from -6 to 6
- new_values: bfloat16 [128, 3, 1024], P(('groups', 'page', 'sub'), None, 'head'), parts along dimension 0, may hold values from -6 to 6
- path_owner: int32 [128, 3], P(('groups', 'page', 'sub')), parts along dimension 0, may hold values from 0 to 7, all different within a row; in each aligned block of 8 rows (0 to 7, 8 to 15, ...) at most 6 rows name the same one
- path_slot: int32 [128, 3], P(('groups', 'page', 'sub')), parts along dimension 0, may hold values from 0 to 7
Outputs:
- attended: bfloat16 [128, 3, 16384], P(('groups', 'page', 'sub'), None, 'head'), parts along dimension 0
The draws below stay inside these ranges and needn't reach their ends.
There are 2 independent parts, one for each index of `groups`. The reference program is written for one: setup_inputs(seed, part) draws one part's arguments, and reference() takes and returns one part's arrays. A program takes and returns all parts, laid end to end along the dimension named above; each array names one. Nothing has to cross between parts.
Inputs may be any that keep to these rules, and one draw needn't show every extreme that they name: `path_owner`: each request names 3 different owners; the requests of one device (aligned blocks of 8 requests) name one owner at most 6 times.
All inputs are finite; a program needn't handle non-finite values.
Results may differ from the reference program's by a relative error of at most 0.0047.
Values may be sent and summed in bfloat16 or wider, within the bound.
A program may use at most 64 MiB of HBM per device.

```python
import math
import jax
import jax.numpy as jnp
import numpy as np
from jax import lax

HD = 128
QH = 128
KVH = 8
GROUP = 16
PAGE_TOK = 128
STEPS = 3
LEVELS = 3
REQ_DEV = 8
PAGE_DEV = 8
REQ = 64
PAGES = 64
CAP = 6
N_PAGE = 8


def paired_keys(key, shape):
    normal_draw = jax.random.normal(key, shape, jnp.float32)
    return jnp.clip(normal_draw, -6.0, 6.0).astype(jnp.bfloat16)


def filled_counts(key, total):
    counts = jax.random.randint(jax.random.fold_in(key, 21), (total,), 1, PAGE_TOK + 1)
    spot = jax.random.randint(jax.random.fold_in(key, 22), (), 0, total)
    return counts.at[spot].set(PAGE_TOK).astype(jnp.int32)


def draw_queries(key, part):
    normal_draw = jax.random.normal(jax.random.fold_in(key, 303), (REQ, STEPS, QH * HD), jnp.float32)
    normal_draw = jnp.clip(normal_draw, -6.0, 6.0) * 2.0
    return jnp.clip(normal_draw, -400.0, 400.0).astype(jnp.bfloat16)


def draw_page_keys(key, part):
    return paired_keys(jax.random.fold_in(key, 101), (PAGES, PAGE_TOK, KVH * HD))


def draw_leaf_keys(key, part):
    return paired_keys(jax.random.fold_in(key, 202), (REQ, PAGE_TOK, KVH * HD))


def draw_page_count(key, part):
    return filled_counts(jax.random.fold_in(key, 405), PAGES)


def draw_leaf_count(key, part):
    return filled_counts(jax.random.fold_in(key, 506), REQ)


def place_ends(result, stream_key, least, top_value):
    shape = result.shape
    index_at = [jax.random.randint(jax.random.fold_in(stream_key, axis), (), 0, shape[axis]) for axis in range(len(shape))]
    result = result.at[tuple(index_at)].set(least)
    longest = shape.index(max(shape))
    index_at[longest] = (index_at[longest] + 1) % shape[longest]
    return result.at[tuple(index_at)].set(top_value)


def level_of(stream_key, dims, split, smallest, top_value):
    loudness = 1.0
    for axis_at, parts in split:
        steps = jax.random.uniform(jax.random.fold_in(jax.random.fold_in(stream_key, 6), axis_at), (parts,), jnp.float32, smallest / len(split), top_value / len(split))
        loudness = loudness * jnp.repeat(jnp.exp(steps), dims[axis_at] // parts).reshape((-1,) + (1,) * (len(dims) - 1 - axis_at))
    return loudness


def shared_out(rng, own, number, rows, amount, top, bound, skew):
    order = jax.random.permutation(rng, amount)
    crowded, usual = shares(amount, rows * top, bound, skew, True), shares(amount, rows * top, bound, skew, False)
    places = jnp.arange(amount)

    def named(sizes, rotation):
        used = int((sizes > 0).sum())
        fixed = max(1, used // 4)
        passed = fixed + (places - fixed + rotation * (used - fixed)) % max(1, amount - fixed)
        return jnp.zeros((amount,), jnp.int32).at[order[jnp.where(places < fixed, places, passed)]].set(jnp.asarray(sizes, jnp.int32))

    sizes = jnp.where(number % 4 == 0, named(crowded, number // 4), named(usual, number - number // 4 - 1))
    mixed = jax.random.permutation(jax.random.fold_in(own, 3), amount)
    giver, receiver = mixed[0:amount // 2 * 2:2], mixed[1:amount // 2 * 2:2]
    margin = jnp.minimum(sizes[giver] - 1, bound - sizes[receiver]) // 2
    margin = jnp.where((giver == order[0]) | (receiver == order[0]) | (sizes[receiver] == 0), 0, jnp.maximum(margin, 0))
    passed = jax.random.randint(jax.random.fold_in(own, 4), (amount // 2,), 0, 1 << 20) % (margin + 1)
    sizes = sizes.at[giver].add(-passed).at[receiver].add(passed)
    labels = jnp.searchsorted(jnp.cumsum(sizes), jnp.arange(rows * top), side="right").astype(jnp.int32)
    table = labels.reshape(top, rows).T
    table = table[jax.random.permutation(jax.random.fold_in(own, 1), rows)]
    rotation = jax.random.randint(jax.random.fold_in(own, 2), (rows, 1), 0, top)
    return jnp.take_along_axis(table, (jnp.arange(top)[None, :] + rotation) % top, axis=1)


def shares(number_of, total, reach, skew, full):
    weights = [(1 << 20) // math.isqrt(grade ** skew) + 1 for grade in range(1, number_of + 1)]
    largest = reach if full else min(reach, max(-(-total // number_of), total * weights[0] // sum(weights)))
    least = 1 if total - largest >= number_of - 1 else 0
    holding, surplus = [largest] + [least] * (number_of - 1), total - largest - least * (number_of - 1)
    while surplus > 0:
        free = [i for i in range(1, number_of) if holding[i] < largest] or [i for i in range(1, number_of) if holding[i] < reach]
        whole, remaining = sum([weights[i] for i in free]), surplus
        for i in free:
            more = min(reach - holding[i], max(1, remaining * weights[i] // whole), surplus)
            holding[i] = holding[i] + more
            surplus = surplus - more
    return np.array(holding)


def noise(own_key, dims, deviation, limit, shards=(), kind=jnp.bfloat16):
    loudness = level_of(own_key, dims, shards, -0.22, 0.18) if shards else 1.0
    values = jax.random.normal(own_key, dims, jnp.float32) * deviation * loudness
    return jnp.minimum(jnp.maximum(values, -limit), limit).astype(kind)


def setup_inputs(seed: int = 0, part: int = 0) -> dict:
    splits = jax.random.split(jax.random.key(seed), 12)
    own_keys = jax.random.split(jax.random.fold_in(splits[11], part), 12)
    queries = draw_queries(jax.random.fold_in(jax.random.fold_in(splits[11], part), 71), part)
    page_keys = draw_page_keys(jax.random.fold_in(jax.random.fold_in(splits[11], part), 71), part)
    page_values = noise(own_keys[2], (PAGES, PAGE_TOK, KVH * HD), 1.0, 6.0, ((0, 8), (2, 2)))
    page_count = draw_page_count(jax.random.fold_in(jax.random.fold_in(splits[11], part), 71), part)
    leaf_keys = draw_leaf_keys(jax.random.fold_in(jax.random.fold_in(splits[11], part), 71), part)
    leaf_values = noise(own_keys[5], (REQ, PAGE_TOK, KVH * HD), 1.0, 6.0, ((0, 8), (2, 2)))
    leaf_count = draw_leaf_count(jax.random.fold_in(jax.random.fold_in(splits[11], part), 71), part)
    new_keys = noise(own_keys[7], (REQ, STEPS, KVH * HD), 1.0, 6.0, ((0, 8), (2, 2)))
    new_values = noise(own_keys[8], (REQ, STEPS, KVH * HD), 1.0, 6.0, ((0, 8), (2, 2)))
    path_owner_keys = jax.random.split(jax.random.fold_in(own_keys[9], 1), REQ // REQ_DEV)
    path_owner_turns = jax.random.permutation(jax.random.fold_in(own_keys[9], 3), REQ // REQ_DEV)
    path_owner = jax.vmap(lambda own, number: shared_out(jax.random.fold_in(own_keys[9], 2), own, number, REQ_DEV, N_PAGE, LEVELS, CAP, 2))(path_owner_keys, path_owner_turns).reshape((REQ, LEVELS))
    path_slot = place_ends(jax.random.randint(own_keys[10], (REQ, LEVELS), 0, PAGE_DEV), jax.random.fold_in(own_keys[10], 1), 0, PAGE_DEV - 1).astype(jnp.int32)
    return {"queries": queries, "page_keys": page_keys, "page_values": page_values, "page_count": page_count, "leaf_keys": leaf_keys, "leaf_values": leaf_values, "leaf_count": leaf_count, "new_keys": new_keys, "new_values": new_values, "path_owner": path_owner, "path_slot": path_slot}


def settle(weights):
    return lax.optimization_barrier(weights.astype(jnp.bfloat16)).astype(jnp.float32)

def reference(queries, page_keys, page_values, page_count, leaf_keys, leaf_values, leaf_count, new_keys, new_values, path_owner, path_slot):
    score_scale = 1.0 / math.sqrt(HD)
    block_rows = REQ_DEV
    block_total = REQ // block_rows
    page_index = (path_owner * PAGE_DEV + path_slot).astype(jnp.int32)

    def shaped(array):
        return array.reshape((block_total, block_rows) + array.shape[1:])

    def per_block(packed):
        query_rows, leaf_key_rows, leaf_value_rows, leaf_length, fresh_keys, fresh_values, wanted = packed
        query_five = query_rows.astype(jnp.float32).reshape(block_rows, STEPS, KVH, GROUP, HD)
        page_key_rows = jnp.take(page_keys, wanted, axis=0).astype(jnp.float32).reshape(block_rows, LEVELS, PAGE_TOK, KVH, HD)
        page_value_rows = jnp.take(page_values, wanted, axis=0).astype(jnp.float32).reshape(block_rows, LEVELS, PAGE_TOK, KVH, HD)
        lengths = jnp.take(page_count, wanted, axis=0)
        token_pos = jnp.arange(PAGE_TOK, dtype=jnp.int32)
        scores = jnp.einsum('bskgd,bltkd->blskgt', query_five, page_key_rows) * score_scale
        allowed = (token_pos[None, None, :] < lengths[:, :, None])[:, :, None, None, None, :]
        scores = jnp.where(allowed, scores, -jnp.inf)
        item_max = lax.optimization_barrier(jnp.max(scores, axis=-1))
        weights = jnp.exp(scores - item_max[..., None])
        item_total = lax.optimization_barrier(jnp.sum(weights, axis=-1))
        item_out = jnp.einsum('blskgt,bltkd->blskgd', settle(weights), page_value_rows) / item_total[..., None]
        item_out = settle(item_out)
        leaf_five = leaf_key_rows.astype(jnp.float32).reshape(block_rows, PAGE_TOK, KVH, HD)
        leaf_vfive = leaf_value_rows.astype(jnp.float32).reshape(block_rows, PAGE_TOK, KVH, HD)
        fresh_five = fresh_keys.astype(jnp.float32).reshape(block_rows, STEPS, KVH, HD)
        fresh_vfive = fresh_values.astype(jnp.float32).reshape(block_rows, STEPS, KVH, HD)
        leaf_scores = jnp.einsum('bskgd,btkd->bskgt', query_five, leaf_five) * score_scale
        leaf_allowed = token_pos[None, :] < leaf_length[:, None]
        leaf_scores = jnp.where(leaf_allowed[:, None, None, None, :], leaf_scores, -jnp.inf)
        fresh_scores = jnp.einsum('bskgd,bukd->bskgu', query_five, fresh_five) * score_scale
        causal = jnp.arange(STEPS, dtype=jnp.int32)[None, :] <= jnp.arange(STEPS, dtype=jnp.int32)[:, None]
        fresh_scores = jnp.where(causal[None, :, None, None, :], fresh_scores, -jnp.inf)
        local_max = jnp.maximum(lax.optimization_barrier(jnp.max(leaf_scores, axis=-1)), lax.optimization_barrier(jnp.max(fresh_scores, axis=-1)))
        leaf_weights = jnp.exp(leaf_scores - local_max[..., None])
        fresh_weights = jnp.exp(fresh_scores - local_max[..., None])
        local_total = lax.optimization_barrier(jnp.sum(leaf_weights, axis=-1)) + lax.optimization_barrier(jnp.sum(fresh_weights, axis=-1))
        local_out = (jnp.einsum('bskgt,btkd->bskgd', settle(leaf_weights), leaf_vfive) + jnp.einsum('bskgu,bukd->bskgd', settle(fresh_weights), fresh_vfive)) / local_total[..., None]
        top_score = jnp.maximum(local_max, lax.optimization_barrier(jnp.max(item_max, axis=1)))
        local_mass = local_total * jnp.exp(local_max - top_score)
        item_mass = item_total * jnp.exp(item_max - top_score[:, None])
        numerator = local_mass[..., None] * local_out + lax.optimization_barrier(jnp.sum(item_mass[..., None] * item_out, axis=1))
        denominator = local_mass + lax.optimization_barrier(jnp.sum(item_mass, axis=1))
        return (numerator / denominator[..., None]).astype(jnp.bfloat16).reshape(block_rows, STEPS, QH * HD)
    outcome = lax.map(per_block, (shaped(queries), shaped(leaf_keys), shaped(leaf_values), shaped(leaf_count), shaped(new_keys), shaped(new_values), shaped(page_index)))
    return outcome.reshape(REQ, STEPS, QH * HD)
```

```python
import functools
import math

import jax
import jax.numpy as jnp
from jax import lax
from jax.experimental import pallas as pl
from jax.experimental.pallas import tpu as pltpu
from jax.sharding import PartitionSpec as P

HD = 128
QH = 128
KVH = 8
NEG = -1e30
MESH = pl.DeviceIdType.MESH


def kernel(
    cfg,
    q_ref,
    pk_hbm,
    pv_hbm,
    lk_hbm,
    lv_hbm,
    nk_ref,
    nv_ref,
    meta_hbm,
    out_ref,
    qbuf,
    kbuf,
    vbuf,
    lkbuf,
    lvbuf,
    mbuf,
    msm,
    pout,
    sout,
    pin,
    sin,
    loc_o,
    loc_s,
    q_send,
    q_recv,
    po_send,
    po_recv,
    ps_send,
    ps_recv,
    page_send,
    page_recv,
    page_local,
    leaf_local,
    meta_send,
    meta_recv,
    meta_local,
):
    lanes, nodes, reqs, kv, rows, steps, levels, tok, rp, groups, offset = cfg
    scale = math.log2(math.e) / math.sqrt(HD)
    me = lax.axis_index("page")
    lane = lax.rem(me, lanes)
    z = lax.div(me, lanes)
    zr = nodes - 1 - z
    pieces = reqs // rp
    per_group = pieces // groups

    def dev(node):
        return {"page": node * lanes + lane}

    partner = z * lanes + (lanes - 1 - lane)

    barrier = pltpu.get_barrier_semaphore()
    for k in range(1, nodes):
        pl.semaphore_signal(
            barrier, inc=1, device_id=dev(lax.rem(z + k, nodes)), device_id_type=MESH
        )
    if lanes > 1:
        pl.semaphore_signal(barrier, inc=1, device_id={"page": partner}, device_id_type=MESH)
    pl.semaphore_wait(barrier, nodes - 1 + lanes - 1)

    def q_copy(direction, src_node, i, own):
        rows_at = pl.ds(i * rp, rp)
        to = z + 1 if direction == 0 else z - 1
        src = q_ref.at[rows_at] if own else qbuf.at[src_node, rows_at]
        return pltpu.make_async_remote_copy(
            src_ref=src,
            dst_ref=qbuf.at[src_node, rows_at],
            send_sem=q_send.at[direction, src_node, i],
            recv_sem=q_recv.at[src_node, i],
            device_id=dev(to),
            device_id_type=MESH,
        )

    def p_copies(direction, d, i):
        rows_at = pl.ds(i * rp, rp)
        to = z + 1 if direction == 0 else z - 1
        slot = d if direction == 0 else jnp.where(d == z - 1, nodes, d)
        return (
            pltpu.make_async_remote_copy(
                src_ref=pout.at[d, rows_at],
                dst_ref=pin.at[slot, rows_at],
                send_sem=po_send.at[d, i],
                recv_sem=po_recv.at[slot, i],
                device_id=dev(to),
                device_id_type=MESH,
            ),
            pltpu.make_async_remote_copy(
                src_ref=sout.at[d, rows_at],
                dst_ref=sin.at[slot, rows_at],
                send_sem=ps_send.at[d, i],
                recv_sem=ps_recv.at[slot, i],
                device_id=dev(to),
                device_id_type=MESH,
            ),
        )

    def wait_p(slot, i):
        rows_at = pl.ds(i * rp, rp)
        pltpu.make_async_copy(pin.at[slot, rows_at], pin.at[slot, rows_at], po_recv.at[slot, i]).wait()
        pltpu.make_async_copy(sin.at[slot, rows_at], sin.at[slot, rows_at], ps_recv.at[slot, i]).wait()

    def wait_q(src_node, i):
        rows_at = pl.ds(i * rp, rp)
        pltpu.make_async_copy(
            qbuf.at[src_node, rows_at], qbuf.at[src_node, rows_at], q_recv.at[src_node, i]
        ).wait()

    def meta_copy(k):
        return pltpu.make_async_remote_copy(
            src_ref=meta_hbm,
            dst_ref=mbuf.at[me],
            send_sem=meta_send.at[k],
            recv_sem=meta_recv.at[me],
            device_id=dev(lax.rem(z + k, nodes)) if k < nodes else {"page": partner},
            device_id_type=MESH,
        )

    meta_count = nodes if lanes > 1 else nodes - 1
    for k in range(1, meta_count + 1):
        meta_copy(k).start()

    @pl.loop(0, pieces)
    def _(i):
        @pl.when(z + 1 < nodes)
        def _():
            q_copy(0, z, i, True).start()

        @pl.when(z > 0)
        def _():
            q_copy(1, z, i, True).start()

    def page_copies():
        return (
            pltpu.make_async_remote_copy(
                src_ref=pk_hbm,
                dst_ref=kbuf.at[lane],
                send_sem=page_send.at[0],
                recv_sem=page_recv.at[0],
                device_id={"page": partner},
                device_id_type=MESH,
            ),
            pltpu.make_async_remote_copy(
                src_ref=pv_hbm,
                dst_ref=vbuf.at[lane],
                send_sem=page_send.at[1],
                recv_sem=page_recv.at[1],
                device_id={"page": partner},
                device_id_type=MESH,
            ),
        )

    if lanes > 1:
        for copy in page_copies():
            copy.start()
    local_copies = (
        pltpu.make_async_copy(pk_hbm, kbuf.at[lane], page_local.at[0]),
        pltpu.make_async_copy(pv_hbm, vbuf.at[lane], page_local.at[1]),
        pltpu.make_async_copy(lk_hbm, lkbuf, leaf_local.at[0]),
        pltpu.make_async_copy(lv_hbm, lvbuf, leaf_local.at[1]),
        pltpu.make_async_copy(meta_hbm, msm.at[me], meta_local.at[0]),
    )
    for copy in local_copies:
        copy.start()

    @pl.when(z == 0)
    def _():
        @pl.loop(0, nodes)
        def _(d):
            @pl.loop(0, reqs)
            def _(r):
                pin[d, r] = jnp.zeros((kv * rows, HD), jnp.bfloat16)
                sin[d, r] = jnp.full((8, 128), NEG, jnp.float32)

    @pl.when(zr == 0)
    def _():
        @pl.loop(0, nodes)
        def _(d):
            slot = jnp.where(d == nodes - 1, nodes, d)

            @pl.loop(0, reqs)
            def _(r):
                pin[slot, r] = jnp.zeros((kv * rows, HD), jnp.bfloat16)
                sin[slot, r] = jnp.full((8, 128), NEG, jnp.float32)

    def take_meta(page_at, k):
        pltpu.make_async_copy(mbuf.at[page_at], mbuf.at[page_at], meta_recv.at[page_at]).wait()
        copy = pltpu.make_async_copy(mbuf.at[page_at], msm.at[page_at], meta_local.at[k])
        copy.start()
        return copy

    taken = [
        take_meta(lax.rem(z + k, nodes) * lanes + lane, k) for k in range(1, nodes)
    ]
    if lanes > 1:
        taken.append(take_meta(partner, nodes))
    for copy in taken:
        copy.wait()
    for copy in local_copies:
        copy.wait()
    if lanes > 1:
        for copy in page_copies():
            copy.wait_recv()

    eye = lax.broadcasted_iota(jnp.int32, (rows, 128), 0) == lax.broadcasted_iota(
        jnp.int32, (rows, 128), 1
    )
    token = lax.broadcasted_iota(jnp.int32, (rows, tok), 1)

    def to_column(row):
        return jnp.sum(
            jnp.where(eye, jnp.broadcast_to(row, (rows, 128)), 0.0), axis=1, keepdims=True
        )

    def to_row(column):
        return jnp.sum(
            jnp.where(eye, jnp.broadcast_to(column, (rows, 128)), 0.0), axis=0, keepdims=True
        )

    def scores_of(query, keys):
        return (
            lax.dot_general(
                query, keys, (((1,), (1,)), ((), ())), preferred_element_type=jnp.float32
            )
            * scale
        )

    def page_of(node, r):
        found = []
        for o in range(lanes):
            owner = z * lanes + o
            slot = jnp.int32(0)
            hit = jnp.int32(0)
            for j in range(levels):
                match = msm[node * lanes + lane, r, j] == owner
                slot = jnp.where(match, msm[node * lanes + lane, r, levels + j], slot)
                hit = jnp.where(match, 1, hit)
            found.append((slot, hit * msm[owner, slot, 2 * levels]))
        return found

    def page_scores(query, pages, h):
        cols = pl.ds(h * HD, HD)
        return [
            jnp.where(token < count, scores_of(query, kbuf[o, slot, :, cols]), NEG)
            for o, (slot, count) in enumerate(pages)
        ]

    def attend(parts, values):
        top = functools.reduce(jnp.maximum, [jnp.max(s, axis=1, keepdims=True) for s in parts])
        total = None
        acc = None
        for s, v in zip(parts, values):
            w = jnp.exp2(s - top)
            part_total = jnp.sum(w, axis=1, keepdims=True)
            part = jnp.dot(w.astype(jnp.bfloat16), v, preferred_element_type=jnp.float32)
            total = part_total if total is None else total + part_total
            acc = part if acc is None else acc + part
        return acc, top, total

    def partial(d, r):
        pages = page_of(d, r)
        stats = []
        for h in range(kv):
            cols = pl.ds(h * HD, HD)
            at = pl.ds(h * rows, rows)
            query = qbuf[d, r, at, :]
            acc, top, total = attend(
                page_scores(query, pages, h), [vbuf[o, p[0], :, cols] for o, p in enumerate(pages)]
            )
            came = to_column(sin[d, r, pl.ds(h, 1), :])
            peak = jnp.maximum(top, came)
            a = jnp.exp2(top - peak)
            b = jnp.exp2(came - peak)
            mass = a * total + b
            inv = 1.0 / mass
            pout[d, r, at, :] = (
                acc * (a * inv) + pin[d, r, at, :].astype(jnp.float32) * (b * inv)
            ).astype(jnp.bfloat16)
            stats.append(to_row(peak + jnp.log2(mass)))
        for h in range(kv):
            sout[d, r, pl.ds(h, 1), :] = stats[h]

    new_pad = nk_ref.shape[1]
    new_token = lax.broadcasted_iota(jnp.int32, (rows, new_pad), 1)
    row_step = lax.broadcasted_iota(jnp.int32, (rows, new_pad), 0) // (rows // steps)

    def local(r):
        pages = page_of(z, r)
        leaf_len = msm[me, r, 2 * levels + 1]
        for h in range(kv):
            cols = pl.ds(h * HD, HD)
            at = pl.ds(h * rows, rows)
            query = q_ref[r, at, :]
            parts = page_scores(query, pages, h)
            values = [vbuf[o, p[0], :, cols] for o, p in enumerate(pages)]
            parts.append(jnp.where(token < leaf_len, scores_of(query, lkbuf[r, :, cols]), NEG))
            values.append(lvbuf[r, :, cols])
            parts.append(
                jnp.where(new_token <= row_step, scores_of(query, nk_ref[r, :, cols]), NEG)
            )
            values.append(nv_ref[r, :, cols])
            acc, top, total = attend(parts, values)
            loc_o[r, at, :] = acc * (1.0 / total)
            loc_s[r, pl.ds(h, 1), :] = to_row(top + jnp.log2(total))

    def final(r):
        for h in range(kv):
            at = pl.ds(h * rows, rows)
            own = to_column(loc_s[r, pl.ds(h, 1), :])
            below = to_column(sin[z, r, pl.ds(h, 1), :])
            above = to_column(sin[nodes, r, pl.ds(h, 1), :])
            peak = jnp.maximum(own, jnp.maximum(below, above))
            a = jnp.exp2(own - peak)
            b = jnp.exp2(below - peak)
            c = jnp.exp2(above - peak)
            inv = 1.0 / (a + b + c)
            out_ref[r, at, :] = (
                loc_o[r, at, :] * (a * inv)
                + pin[z, r, at, :].astype(jnp.float32) * (b * inv)
                + pin[nodes, r, at, :].astype(jnp.float32) * (c * inv)
            ).astype(jnp.bfloat16)

    local_step = jnp.where((z == 0) | (zr == 0), nodes, min(2, nodes))

    def piece_work(t, i):
        below = z - t
        above = z + t

        @pl.when(below >= 0)
        def _():
            wait_q(below, i)

            @pl.when(z + 1 < nodes)
            def _():
                q_copy(0, below, i, False).start()

        @pl.when(above < nodes)
        def _():
            wait_q(above, i)

            @pl.when(z > 0)
            def _():
                q_copy(1, above, i, False).start()

        up = t - z

        @pl.when((up > z) & (up < nodes))
        def _():
            @pl.when(z > 0)
            def _():
                wait_p(up, i)

            for j in range(rp):
                partial(up, i * rp + j)
            for copy in p_copies(0, up, i):
                copy.start()

        down = t - zr

        @pl.when((down > zr) & (down < nodes))
        def _():
            d = nodes - 1 - down

            @pl.when(zr > 0)
            def _():
                wait_p(d, i)

            for j in range(rp):
                partial(d, i * rp + j)
            for copy in p_copies(1, d, i):
                copy.start()

        @pl.when(t == local_step)
        def _():
            for j in range(rp):
                local(i * rp + j)

    last = 2 * nodes - 2

    @pl.loop(1, last + 1 + offset * (groups - 1))
    def _(tau):
        for g in range(groups):
            t = tau - offset * g

            @pl.when((t >= 1) & (t <= last))
            def _():
                @pl.loop(g * per_group, (g + 1) * per_group)
                def _(i):
                    piece_work(t, i)

    @pl.loop(0, pieces)
    def _(i):
        @pl.when(z > 0)
        def _():
            wait_p(z, i)

        @pl.when(zr > 0)
        def _():
            wait_p(nodes, i)

        for j in range(rp):
            final(i * rp + j)

    for k in range(1, meta_count + 1):
        meta_copy(k).wait_send()
    if lanes > 1:
        for copy in page_copies():
            copy.wait_send()

    @pl.loop(0, pieces)
    def _(i):
        @pl.when(z + 1 < nodes)
        def _():
            q_copy(0, z, i, True).wait_send()

        @pl.when(z > 0)
        def _():
            q_copy(1, z, i, True).wait_send()

        @pl.loop(0, nodes)
        def _(n):
            @pl.when((n < z) & (z + 1 < nodes))
            def _():
                q_copy(0, n, i, False).wait_send()

            @pl.when((n > z) & (z > 0))
            def _():
                q_copy(1, n, i, False).wait_send()

            @pl.when(n > z)
            def _():
                for copy in p_copies(0, n, i):
                    copy.wait_send()

            @pl.when(n < z)
            def _():
                for copy in p_copies(1, n, i):
                    copy.wait_send()


def shards(
    queries,
    page_keys,
    page_values,
    page_count,
    leaf_keys,
    leaf_values,
    leaf_count,
    new_keys,
    new_values,
    path_owner,
    path_slot,
    lanes,
):
    reqs, steps, head_width = queries.shape
    pages, tok, kv_width = page_keys.shape
    kv = kv_width // HD
    group = QH // KVH
    rows = steps * group
    levels = path_owner.shape[1]
    owners = lax.axis_size("page")
    nodes = owners // lanes
    small = nodes <= 8
    rp = 1 if small else reqs
    groups = GROUPS if small else 1
    offset = nodes
    query_rows = (
        queries.reshape(reqs, steps, kv, group, HD)
        .transpose(0, 2, 1, 3, 4)
        .reshape(reqs, kv * rows, HD)
    )
    new_pad = 16
    pad = ((0, 0), (0, new_pad - steps), (0, 0))
    fresh_keys = jnp.pad(new_keys, pad)
    fresh_values = jnp.pad(new_values, pad)
    meta_rows = max(reqs, pages)
    parts = [path_owner, path_slot, page_count[:, None], leaf_count[:, None]]
    meta = jnp.concatenate(
        [jnp.pad(p, ((0, meta_rows - p.shape[0]), (0, 0))) for p in parts], axis=1
    )
    meta = jnp.pad(meta, ((0, 0), (0, 128 - meta.shape[1])))
    cfg = (lanes, nodes, reqs, kv, rows, steps, levels, tok, rp, groups, offset)
    pieces = reqs // rp
    vmem = pl.BlockSpec(memory_space=pltpu.VMEM)
    hbm = pl.BlockSpec(memory_space=pl.ANY)
    dma = pltpu.SemaphoreType.DMA
    block = (reqs, kv * rows, HD)
    stat = (reqs, 8, 128)
    out = pl.pallas_call(
        functools.partial(kernel, cfg),
        out_shape=jax.ShapeDtypeStruct(block, jnp.bfloat16),
        in_specs=[vmem, hbm, hbm, hbm, hbm, vmem, vmem, hbm],
        out_specs=vmem,
        scratch_shapes=[
            pltpu.VMEM((nodes,) + block, jnp.bfloat16),
            pltpu.VMEM((lanes,) + page_keys.shape, jnp.bfloat16),
            pltpu.VMEM((lanes,) + page_keys.shape, jnp.bfloat16),
            pltpu.VMEM(leaf_keys.shape, jnp.bfloat16),
            pltpu.VMEM(leaf_keys.shape, jnp.bfloat16),
            pltpu.VMEM((owners, meta_rows, 128), jnp.int32),
            pltpu.SMEM((owners, meta_rows, 128), jnp.int32),
            pltpu.VMEM((nodes,) + block, jnp.bfloat16),
            pltpu.VMEM((nodes,) + stat, jnp.float32),
            pltpu.VMEM((nodes + 1,) + block, jnp.bfloat16),
            pltpu.VMEM((nodes + 1,) + stat, jnp.float32),
            pltpu.VMEM(block, jnp.float32),
            pltpu.VMEM(stat, jnp.float32),
            dma((2, nodes, pieces)),
            dma((nodes, pieces)),
            dma((nodes, pieces)),
            dma((nodes + 1, pieces)),
            dma((nodes, pieces)),
            dma((nodes + 1, pieces)),
            dma((2,)),
            dma((2,)),
            dma((2,)),
            dma((2,)),
            dma((nodes + 1,)),
            dma((owners,)),
            dma((nodes + 1,)),
        ],
        compiler_params=pltpu.CompilerParams(
            collective_id=0, has_side_effects=True, vmem_limit_bytes=60 * 1024 * 1024
        ),
    )(
        query_rows,
        page_keys,
        page_values,
        leaf_keys,
        leaf_values,
        fresh_keys,
        fresh_values,
        meta,
    )
    return (
        out.reshape(reqs, kv, steps, group, HD)
        .transpose(0, 2, 1, 3, 4)
        .reshape(reqs, steps, head_width)
    )


GROUPS = 1


def solution(mesh):
    lanes = 2 if mesh.shape["sub"] == 1 and mesh.shape["page"] % 4 == 0 else 1
    return jax.shard_map(
        functools.partial(shards, lanes=lanes),
        mesh=mesh,
        in_specs=(
            P(("groups", "page", "sub"), None, "head"),
            P(("groups", "page"), None, "head"),
            P(("groups", "page"), None, "head"),
            P(("groups", "page")),
            P(("groups", "page", "sub"), None, "head"),
            P(("groups", "page", "sub"), None, "head"),
            P(("groups", "page", "sub")),
            P(("groups", "page", "sub"), None, "head"),
            P(("groups", "page", "sub"), None, "head"),
            P(("groups", "page", "sub"), None),
            P(("groups", "page", "sub"), None),
        ),
        out_specs=P(("groups", "page", "sub"), None, "head"),
        check_vma=False,
    )
```

```python
import functools
import math

import jax
import jax.numpy as jnp
from jax import lax
from jax.experimental import pallas as pl
from jax.experimental.pallas import tpu as pltpu
from jax.sharding import PartitionSpec as P

HD = 128
QH = 128
KVH = 8
NEG = -1e30
MESH = pl.DeviceIdType.MESH


def kernel(
    cfg,
    q_ref,
    pk_hbm,
    pv_hbm,
    lk_hbm,
    lv_hbm,
    nk_ref,
    nv_ref,
    owner_hbm,
    slot_hbm,
    count_hbm,
    leaf_hbm,
    out_ref,
    qbuf,
    kbuf,
    vbuf,
    lkbuf,
    lvbuf,
    mbuf,
    msm,
    leaf_sm,
    fresh_k,
    fresh_v,
    pout,
    pin,
    loc_o,
    loc_s,
    q_send,
    q_recv,
    po_send,
    po_recv,
    page_send,
    page_recv,
    page_local,
    leaf_local,
    meta_send,
    meta_recv,
    meta_local,
):
    lanes, nodes, reqs, kv, rows, steps, levels, tok, rp, lag, hold, end_local, mid_local = cfg
    scale = math.log2(math.e) / math.sqrt(HD)
    me = lax.axis_index("page")
    lane = lax.rem(me, lanes)
    z = lax.div(me, lanes)
    zr = nodes - 1 - z
    pieces = reqs // rp

    def dev(node):
        return {"page": node * lanes + lane}

    partner = z * lanes + (lanes - 1 - lane)

    barrier = pltpu.get_barrier_semaphore()
    for k in range(1, nodes):
        pl.semaphore_signal(
            barrier, inc=1, device_id=dev(lax.rem(z + k, nodes)), device_id_type=MESH
        )
    if lanes > 1:
        pl.semaphore_signal(barrier, inc=1, device_id={"page": partner}, device_id_type=MESH)
    pl.semaphore_wait(barrier, nodes - 1 + lanes - 1)

    def q_copy(direction, src_node, i, own):
        rows_at = pl.ds(i * rp, rp)
        to = z + 1 if direction == 0 else z - 1
        src = q_ref.at[rows_at] if own else qbuf.at[src_node, rows_at]
        return pltpu.make_async_remote_copy(
            src_ref=src,
            dst_ref=qbuf.at[src_node, rows_at],
            send_sem=q_send.at[direction, src_node, i],
            recv_sem=q_recv.at[src_node, i],
            device_id=dev(to),
            device_id_type=MESH,
        )

    def p_copy(direction, d, i):
        rows_at = pl.ds(i * rp, rp)
        to = z + 1 if direction == 0 else z - 1
        slot = d if direction == 0 else jnp.where(d == z - 1, nodes, d)
        return pltpu.make_async_remote_copy(
            src_ref=pout.at[d, rows_at],
            dst_ref=pin.at[slot, rows_at],
            send_sem=po_send.at[d, i],
            recv_sem=po_recv.at[slot, i],
            device_id=dev(to),
            device_id_type=MESH,
        )

    def wait_p(slot, i):
        rows_at = pl.ds(i * rp, rp)
        pltpu.make_async_copy(pin.at[slot, rows_at], pin.at[slot, rows_at], po_recv.at[slot, i]).wait()

    def wait_q(src_node, i):
        rows_at = pl.ds(i * rp, rp)
        pltpu.make_async_copy(
            qbuf.at[src_node, rows_at], qbuf.at[src_node, rows_at], q_recv.at[src_node, i]
        ).wait()

    def meta_copies(k):
        device = dev(lax.rem(z + k, nodes)) if k < nodes else {"page": partner}
        sources = (owner_hbm, slot_hbm) if k < nodes else (count_hbm,)
        return [
            pltpu.make_async_remote_copy(
                src_ref=src,
                dst_ref=mbuf.at[me, pl.ds(n * 8, src.shape[0])],
                send_sem=meta_send.at[k, n],
                recv_sem=meta_recv.at[me, n],
                device_id=device,
                device_id_type=MESH,
            )
            for n, src in enumerate(sources)
        ]

    meta_count = nodes if lanes > 1 else nodes - 1
    for k in range(1, meta_count + 1):
        for copy in meta_copies(k):
            copy.start()

    def page_copies():
        return (
            pltpu.make_async_remote_copy(
                src_ref=pk_hbm,
                dst_ref=kbuf.at[lane],
                send_sem=page_send.at[0],
                recv_sem=page_recv.at[0],
                device_id={"page": partner},
                device_id_type=MESH,
            ),
            pltpu.make_async_remote_copy(
                src_ref=pv_hbm,
                dst_ref=vbuf.at[lane],
                send_sem=page_send.at[1],
                recv_sem=page_recv.at[1],
                device_id={"page": partner},
                device_id_type=MESH,
            ),
        )

    if lanes > 1:
        for copy in page_copies():
            copy.start()
    local_copies = (
        pltpu.make_async_copy(pk_hbm, kbuf.at[lane], page_local.at[0]),
        pltpu.make_async_copy(pv_hbm, vbuf.at[lane], page_local.at[1]),
        pltpu.make_async_copy(lk_hbm, lkbuf, leaf_local.at[0]),
        pltpu.make_async_copy(lv_hbm, lvbuf, leaf_local.at[1]),
        pltpu.make_async_copy(owner_hbm, msm.at[me, pl.ds(0, levels)], meta_local.at[0, 0]),
        pltpu.make_async_copy(slot_hbm, msm.at[me, pl.ds(8, levels)], meta_local.at[0, 1]),
        pltpu.make_async_copy(count_hbm, msm.at[me, pl.ds(16, 1)], meta_local.at[0, 2]),
        pltpu.make_async_copy(leaf_hbm, leaf_sm, meta_local.at[0, 3]),
    )
    for copy in local_copies:
        copy.start()

    stat_row = lax.broadcasted_iota(jnp.int32, (16, 128), 0)
    empty = jnp.where(stat_row < kv, NEG, 0.0).astype(jnp.bfloat16)
    stat_at = pl.ds(kv * rows, 16)
    fresh_k[...] = jnp.zeros_like(fresh_k)
    fresh_v[...] = jnp.zeros_like(fresh_v)
    for n in range(steps):
        fresh_k[n * reqs : (n + 1) * reqs, :] = nk_ref[n]
        fresh_v[n * reqs : (n + 1) * reqs, :] = nv_ref[n]

    @pl.when(z == 0)
    def _():
        @pl.loop(0, nodes)
        def _(d):
            @pl.loop(0, reqs)
            def _(r):
                pin[d, r] = jnp.zeros((kv * rows + 16, HD), jnp.bfloat16)
                pin[d, r, pl.ds(kv * rows, 16), :] = empty

    @pl.when(zr == 0)
    def _():
        @pl.loop(0, nodes)
        def _(d):
            slot = jnp.where(d == nodes - 1, nodes, d)

            @pl.loop(0, reqs)
            def _(r):
                pin[slot, r] = jnp.zeros((kv * rows + 16, HD), jnp.bfloat16)
                pin[slot, r, pl.ds(kv * rows, 16), :] = empty

    def take_meta(page_at, k, heights, first):
        copies = []
        for n, height in enumerate(heights):
            got = mbuf.at[page_at, pl.ds(n * 8, height)]
            pltpu.make_async_copy(got, got, meta_recv.at[page_at, n]).wait()
            copies.append(
                pltpu.make_async_copy(
                    got, msm.at[page_at, pl.ds(first + n * 8, height)], meta_local.at[k, n]
                )
            )
        for copy in copies:
            copy.start()
        return copies

    def settle():
        taken = []
        for k in range(1, nodes):
            taken += take_meta(lax.rem(z + k, nodes) * lanes + lane, k, (levels, levels), 0)
        if lanes > 1:
            taken += take_meta(partner, nodes, (1,), 16)
        for copy in taken:
            copy.wait()
        for copy in local_copies:
            copy.wait()
        if lanes > 1:
            for copy in page_copies():
                copy.wait_recv()

    eye = lax.broadcasted_iota(jnp.int32, (rows, 128), 0) == lax.broadcasted_iota(
        jnp.int32, (rows, 128), 1
    )
    token = lax.broadcasted_iota(jnp.int32, (rows, tok), 1)

    def to_column(row):
        return jnp.sum(
            jnp.where(eye, jnp.broadcast_to(row, (rows, 128)), 0.0), axis=1, keepdims=True
        )

    def to_row(column):
        return jnp.sum(
            jnp.where(eye, jnp.broadcast_to(column, (rows, 128)), 0.0), axis=0, keepdims=True
        )

    def scores_of(query, keys):
        return (
            lax.dot_general(
                query, keys, (((1,), (1,)), ((), ())), preferred_element_type=jnp.float32
            )
            * scale
        )

    def page_of(node, r):
        found = []
        for o in range(lanes):
            owner = z * lanes + o
            slot = jnp.int32(0)
            hit = jnp.int32(0)
            for j in range(levels):
                match = msm[node * lanes + lane, j, r] == owner
                slot = jnp.where(match, msm[node * lanes + lane, 8 + j, r], slot)
                hit = jnp.where(match, 1, hit)
            found.append((slot, hit * msm[owner, 16, slot]))
        return found

    def page_scores(query, pages, h):
        cols = pl.ds(h * HD, HD)
        return [
            jnp.where(token < count, scores_of(query, kbuf[o, slot, :, cols]), NEG)
            for o, (slot, count) in enumerate(pages)
        ]

    def total_max(parts):
        wide = functools.reduce(jnp.maximum, [s for s in parts if s.shape[1] == tok])
        top = jnp.max(wide, axis=1, keepdims=True)
        for s in parts:
            if s.shape[1] != tok:
                top = jnp.maximum(top, jnp.max(s, axis=1, keepdims=True))
        return top

    def total_sum(parts):
        wide = functools.reduce(jnp.add, [w for w in parts if w.shape[1] == tok])
        total = jnp.sum(wide, axis=1, keepdims=True)
        for w in parts:
            if w.shape[1] != tok:
                total = total + jnp.sum(w, axis=1, keepdims=True)
        return total

    def attend(parts, values):
        heads = range(kv)
        tops = [total_max(parts[h]) for h in heads]
        weights = [[jnp.exp2(s - tops[h]) for s in parts[h]] for h in heads]
        accs = [
            functools.reduce(
                jnp.add,
                [
                    jnp.dot(w.astype(jnp.bfloat16), v, preferred_element_type=jnp.float32)
                    for w, v in zip(weights[h], values[h])
                ],
            )
            for h in heads
        ]
        return accs, tops, [total_sum(weights[h]) for h in heads]

    def stat_rows(packed):
        wide = packed.astype(jnp.float32)
        return [
            wide[h : h + 1] + (wide[kv + h : kv + h + 1] + wide[2 * kv + h : 2 * kv + h + 1])
            for h in range(kv)
        ]

    def pack_stats(columns):
        stat = jnp.zeros((16, 128), jnp.float32)
        for h, column in enumerate(columns):
            stat = jnp.where(lax.rem(stat_row, kv) == h, to_row(column), stat)
        first = stat.astype(jnp.bfloat16).astype(jnp.float32)
        rest = stat - first
        second = rest.astype(jnp.bfloat16).astype(jnp.float32)
        third = rest - second
        return jnp.where(
            stat_row < kv, first, jnp.where(stat_row < 2 * kv, second, third)
        ).astype(jnp.bfloat16)

    def span(h):
        return pl.ds(h * rows, rows)

    def partial(d, r):
        pages = page_of(d, r)
        parts = [page_scores(qbuf[d, r, span(h), :], pages, h) for h in range(kv)]
        values = [
            [vbuf[o, p[0], :, pl.ds(h * HD, HD)] for o, p in enumerate(pages)] for h in range(kv)
        ]
        accs, tops, totals = attend(parts, values)
        came = [to_column(row) for row in stat_rows(pin[d, r, stat_at, :])]
        outs, stats = [], []
        for h in range(kv):
            peak = jnp.maximum(tops[h], came[h])
            a = jnp.exp2(tops[h] - peak)
            b = jnp.exp2(came[h] - peak)
            mass = a * totals[h] + b
            inv = 1.0 / mass
            outs.append(
                accs[h] * (a * inv) + pin[d, r, span(h), :].astype(jnp.float32) * (b * inv)
            )
            stats.append(peak + jnp.log2(mass))
        for h in range(kv):
            pout[d, r, span(h), :] = outs[h].astype(jnp.bfloat16)
        pout[d, r, stat_at, :] = pack_stats(stats)

    new_pad = fresh_k.shape[0]
    new_token = lax.broadcasted_iota(jnp.int32, (rows, new_pad), 1)
    row_step = lax.broadcasted_iota(jnp.int32, (rows, new_pad), 0) // (rows // steps)
    causal = new_token // reqs <= row_step

    def local(r):
        pages = page_of(z, r)
        leaf_len = leaf_sm[0, r]
        fresh = causal & (lax.rem(new_token, reqs) == r)
        parts, values = [], []
        for h in range(kv):
            cols = pl.ds(h * HD, HD)
            query = q_ref[r, span(h), :]
            parts.append(
                page_scores(query, pages, h)
                + [
                    jnp.where(token < leaf_len, scores_of(query, lkbuf[r, :, cols]), NEG),
                    jnp.where(fresh, scores_of(query, fresh_k[:, cols]), NEG),
                ]
            )
            values.append(
                [vbuf[o, p[0], :, cols] for o, p in enumerate(pages)]
                + [lvbuf[r, :, cols], fresh_v[:, cols]]
            )
        accs, tops, totals = attend(parts, values)
        for h in range(kv):
            loc_o[r, span(h), :] = accs[h] * (1.0 / totals[h])
            loc_s[r, pl.ds(h, 1), :] = to_row(tops[h] + jnp.log2(totals[h]))

    def final(r):
        below_rows = stat_rows(pin[z, r, stat_at, :])
        above_rows = stat_rows(pin[nodes, r, stat_at, :])
        outs = []
        for h in range(kv):
            own = to_column(loc_s[r, pl.ds(h, 1), :])
            below = to_column(below_rows[h])
            above = to_column(above_rows[h])
            peak = jnp.maximum(own, jnp.maximum(below, above))
            a = jnp.exp2(own - peak)
            b = jnp.exp2(below - peak)
            c = jnp.exp2(above - peak)
            inv = 1.0 / (a + b + c)
            outs.append(
                loc_o[r, span(h), :] * (a * inv)
                + pin[z, r, span(h), :].astype(jnp.float32) * (b * inv)
                + pin[nodes, r, span(h), :].astype(jnp.float32) * (c * inv)
            )
        for h in range(kv):
            out_ref[r, span(h), :] = outs[h].astype(jnp.bfloat16)

    def chain_place(v, pos, delay):
        index = v - lag * pos - delay
        return index, lax.div(index, pieces), lax.rem(index, pieces)

    def query_work(v, direction):
        pos = z if direction == 0 else zr
        index, s, i = chain_place(v, pos, 0)
        src_node = s if direction == 0 else nodes - 1 - s

        @pl.when((index >= 0) & (s < pos))
        def _():
            wait_q(src_node, i)

            @pl.when(pos < nodes - 1)
            def _():
                q_copy(direction, src_node, i, False).start()

        @pl.when((index >= 0) & (s == pos) & (pos < nodes - 1))
        def _():
            q_copy(direction, z, i, True).start()

    def partial_work(v, direction):
        pos = z if direction == 0 else zr
        index, s, i = chain_place(v, pos, hold)
        ahead = nodes + pos - s
        d = ahead if direction == 0 else nodes - 1 - ahead

        @pl.when((index >= 0) & (s > pos) & (s < nodes) & (pos < nodes - 1))
        def _():
            @pl.when(pos > 0)
            def _():
                wait_p(d, i)

            for j in range(rp):
                partial(d, i * rp + j)
            p_copy(direction, d, i).start()

    at_end = (z == 0) | (zr == 0)
    local_at = jnp.where(at_end, end_local, mid_local)
    settle_at = jnp.minimum(local_at, pieces + hold)

    @pl.loop(0, (nodes + 1) * pieces + lag * (nodes - 1) + hold)
    def _(v):
        for direction in range(2):
            query_work(v, direction)

        @pl.when(v == settle_at)
        def _():
            settle()

        for direction in range(2):
            partial_work(v, direction)

        @pl.when((v >= local_at) & (v < local_at + pieces))
        def _():
            for j in range(rp):
                local((v - local_at) * rp + j)

    @pl.loop(0, pieces)
    def _(i):
        @pl.when(z > 0)
        def _():
            wait_p(z, i)

        @pl.when(zr > 0)
        def _():
            wait_p(nodes, i)

        for j in range(rp):
            final(i * rp + j)

    for k in range(1, meta_count + 1):
        for copy in meta_copies(k):
            copy.wait_send()
    if lanes > 1:
        for copy in page_copies():
            copy.wait_send()

    @pl.loop(0, pieces)
    def _(i):
        @pl.when(z + 1 < nodes)
        def _():
            q_copy(0, z, i, True).wait_send()

        @pl.when(z > 0)
        def _():
            q_copy(1, z, i, True).wait_send()

        @pl.loop(0, nodes)
        def _(n):
            @pl.when((n < z) & (z + 1 < nodes))
            def _():
                q_copy(0, n, i, False).wait_send()

            @pl.when((n > z) & (z > 0))
            def _():
                q_copy(1, n, i, False).wait_send()

            @pl.when(n > z)
            def _():
                p_copy(0, n, i).wait_send()

            @pl.when(n < z)
            def _():
                p_copy(1, n, i).wait_send()


def shards(
    queries,
    page_keys,
    page_values,
    page_count,
    leaf_keys,
    leaf_values,
    leaf_count,
    new_keys,
    new_values,
    path_owner,
    path_slot,
    lanes,
):
    reqs, steps, head_width = queries.shape
    pages, tok, kv_width = page_keys.shape
    kv = kv_width // HD
    group = QH // KVH
    rows = steps * group
    levels = path_owner.shape[1]
    owners = lax.axis_size("page")
    nodes = owners // lanes
    small = nodes <= 8
    rp = 1 if small else reqs
    pieces = reqs // rp
    lag = LAG if small else 1
    hold = max(0, lag * (nodes - 1) - pieces)
    mid_local = pieces
    end_local = END_LOCAL * pieces if small else nodes * pieces
    query_rows = (
        queries.reshape(reqs, steps, kv, group, HD)
        .transpose(0, 2, 1, 3, 4)
        .reshape(reqs, kv * rows, HD)
    )
    assert 3 * kv <= 16 and rows <= 128 and levels <= 8
    cfg = (lanes, nodes, reqs, kv, rows, steps, levels, tok, rp, lag, hold, end_local, mid_local)
    vmem = pl.BlockSpec(memory_space=pltpu.VMEM)
    hbm = pl.BlockSpec(memory_space=pl.ANY)
    dma = pltpu.SemaphoreType.DMA
    block = (reqs, kv * rows, HD)
    stat = (reqs, 8, 128)
    sent = (reqs, kv * rows + 16, HD)
    fresh_rows = -(-steps * reqs // 16) * 16
    out = pl.pallas_call(
        functools.partial(kernel, cfg),
        out_shape=jax.ShapeDtypeStruct(block, jnp.bfloat16),
        in_specs=[vmem, hbm, hbm, hbm, hbm, vmem, vmem, hbm, hbm, hbm, hbm],
        out_specs=vmem,
        scratch_shapes=[
            pltpu.VMEM((nodes,) + block, jnp.bfloat16),
            pltpu.VMEM((lanes,) + page_keys.shape, jnp.bfloat16),
            pltpu.VMEM((lanes,) + page_keys.shape, jnp.bfloat16),
            pltpu.VMEM(leaf_keys.shape, jnp.bfloat16),
            pltpu.VMEM(leaf_keys.shape, jnp.bfloat16),
            pltpu.VMEM((owners, 16, pages), jnp.int32),
            pltpu.SMEM((owners, 24, pages), jnp.int32),
            pltpu.SMEM((1, reqs), jnp.int32),
            pltpu.VMEM((fresh_rows, kv_width), jnp.bfloat16),
            pltpu.VMEM((fresh_rows, kv_width), jnp.bfloat16),
            pltpu.VMEM((nodes,) + sent, jnp.bfloat16),
            pltpu.VMEM((nodes + 1,) + sent, jnp.bfloat16),
            pltpu.VMEM(block, jnp.float32),
            pltpu.VMEM(stat, jnp.float32),
            dma((2, nodes, pieces)),
            dma((nodes, pieces)),
            dma((nodes, pieces)),
            dma((nodes + 1, pieces)),
            dma((2,)),
            dma((2,)),
            dma((2,)),
            dma((2,)),
            dma((nodes + 1, 2)),
            dma((owners, 2)),
            dma((nodes + 1, 4)),
        ],
        compiler_params=pltpu.CompilerParams(
            collective_id=0, has_side_effects=True, vmem_limit_bytes=60 * 1024 * 1024
        ),
    )(
        query_rows,
        page_keys,
        page_values,
        leaf_keys,
        leaf_values,
        new_keys.transpose(1, 0, 2),
        new_values.transpose(1, 0, 2),
        path_owner.T,
        path_slot.T,
        page_count[None, :],
        leaf_count[None, :],
    )
    return (
        out.reshape(reqs, kv, steps, group, HD)
        .transpose(0, 2, 1, 3, 4)
        .reshape(reqs, steps, head_width)
    )


LAG = 3
END_LOCAL = 2


def solution(mesh):
    lanes = 2 if mesh.shape["sub"] == 1 and mesh.shape["page"] % 4 == 0 else 1
    return jax.shard_map(
        functools.partial(shards, lanes=lanes),
        mesh=mesh,
        in_specs=(
            P(("groups", "page", "sub"), None, "head"),
            P(("groups", "page"), None, "head"),
            P(("groups", "page"), None, "head"),
            P(("groups", "page")),
            P(("groups", "page", "sub"), None, "head"),
            P(("groups", "page", "sub"), None, "head"),
            P(("groups", "page", "sub")),
            P(("groups", "page", "sub"), None, "head"),
            P(("groups", "page", "sub"), None, "head"),
            P(("groups", "page", "sub"), None),
            P(("groups", "page", "sub"), None),
        ),
        out_specs=P(("groups", "page", "sub"), None, "head"),
        check_vma=False,
    )
```

```python
import functools
import math

import jax
import jax.numpy as jnp
from jax import lax
from jax.experimental import pallas as pl
from jax.experimental.pallas import tpu as pltpu
from jax.sharding import PartitionSpec as P

HD = 128
QH = 128
KVH = 8
NEG = -1e30
MESH = pl.DeviceIdType.MESH


def kernel(
    cfg,
    q_ref,
    pk_hbm,
    pv_hbm,
    lk_hbm,
    lv_hbm,
    nk_ref,
    nv_ref,
    owner_hbm,
    slot_hbm,
    count_hbm,
    leaf_hbm,
    out_ref,
    qbuf,
    kbuf,
    vbuf,
    lkbuf,
    lvbuf,
    mbuf,
    msm,
    leaf_sm,
    fresh_k,
    fresh_v,
    pout,
    pin,
    loc_o,
    loc_s,
    q_send,
    q_recv,
    po_send,
    po_recv,
    page_send,
    page_recv,
    page_local,
    leaf_local,
    meta_send,
    meta_recv,
    meta_local,
):
    lanes, nodes, reqs, kv, rows, steps, levels, tok, rp, lag, hold, end_local, mid_local = cfg
    scale = math.log2(math.e) / math.sqrt(HD)
    me = lax.axis_index("page")
    lane = lax.rem(me, lanes)
    z = lax.div(me, lanes)
    zr = nodes - 1 - z
    pieces = reqs // rp

    def dev(node):
        return {"page": node * lanes + lane}

    partner = z * lanes + (lanes - 1 - lane)

    local_copies = (
        pltpu.make_async_copy(pk_hbm, kbuf.at[lane], page_local.at[0]),
        pltpu.make_async_copy(pv_hbm, vbuf.at[lane], page_local.at[1]),
        pltpu.make_async_copy(lk_hbm, lkbuf, leaf_local.at[0]),
        pltpu.make_async_copy(lv_hbm, lvbuf, leaf_local.at[1]),
        pltpu.make_async_copy(owner_hbm, msm.at[me, pl.ds(0, levels)], meta_local.at[0, 0]),
        pltpu.make_async_copy(slot_hbm, msm.at[me, pl.ds(8, levels)], meta_local.at[0, 1]),
        pltpu.make_async_copy(count_hbm, msm.at[me, pl.ds(16, 1)], meta_local.at[0, 2]),
        pltpu.make_async_copy(leaf_hbm, leaf_sm, meta_local.at[0, 3]),
    )
    for copy in local_copies:
        copy.start()

    barrier = pltpu.get_barrier_semaphore()
    for k in range(1, nodes):
        pl.semaphore_signal(
            barrier, inc=1, device_id=dev(lax.rem(z + k, nodes)), device_id_type=MESH
        )
    if lanes > 1:
        pl.semaphore_signal(barrier, inc=1, device_id={"page": partner}, device_id_type=MESH)
    pl.semaphore_wait(barrier, nodes - 1 + lanes - 1)

    def q_copy(direction, src_node, i, own):
        rows_at = pl.ds(i * rp, rp)
        to = z + 1 if direction == 0 else z - 1
        src = q_ref.at[rows_at] if own else qbuf.at[src_node, rows_at]
        return pltpu.make_async_remote_copy(
            src_ref=src,
            dst_ref=qbuf.at[src_node, rows_at],
            send_sem=q_send.at[direction, src_node, i],
            recv_sem=q_recv.at[src_node, i],
            device_id=dev(to),
            device_id_type=MESH,
        )

    def p_copy(direction, d, i):
        rows_at = pl.ds(i * rp, rp)
        to = z + 1 if direction == 0 else z - 1
        slot = d if direction == 0 else jnp.where(d == z - 1, nodes, d)
        return pltpu.make_async_remote_copy(
            src_ref=pout.at[d, rows_at],
            dst_ref=pin.at[slot, rows_at],
            send_sem=po_send.at[d, i],
            recv_sem=po_recv.at[slot, i],
            device_id=dev(to),
            device_id_type=MESH,
        )

    def wait_p(slot, i):
        rows_at = pl.ds(i * rp, rp)
        pltpu.make_async_copy(pin.at[slot, rows_at], pin.at[slot, rows_at], po_recv.at[slot, i]).wait()

    def wait_q(src_node, i):
        rows_at = pl.ds(i * rp, rp)
        pltpu.make_async_copy(
            qbuf.at[src_node, rows_at], qbuf.at[src_node, rows_at], q_recv.at[src_node, i]
        ).wait()

    def meta_copies(k):
        device = dev(lax.rem(z + k, nodes)) if k < nodes else {"page": partner}
        sources = (owner_hbm, slot_hbm) if k < nodes else (count_hbm,)
        return [
            pltpu.make_async_remote_copy(
                src_ref=src,
                dst_ref=mbuf.at[me, pl.ds(n * 8, src.shape[0])],
                send_sem=meta_send.at[k, n],
                recv_sem=meta_recv.at[me, n],
                device_id=device,
                device_id_type=MESH,
            )
            for n, src in enumerate(sources)
        ]

    meta_count = nodes if lanes > 1 else nodes - 1
    for k in range(1, meta_count + 1):
        for copy in meta_copies(k):
            copy.start()

    def page_copies():
        return (
            pltpu.make_async_remote_copy(
                src_ref=pk_hbm,
                dst_ref=kbuf.at[lane],
                send_sem=page_send.at[0],
                recv_sem=page_recv.at[0],
                device_id={"page": partner},
                device_id_type=MESH,
            ),
            pltpu.make_async_remote_copy(
                src_ref=pv_hbm,
                dst_ref=vbuf.at[lane],
                send_sem=page_send.at[1],
                recv_sem=page_recv.at[1],
                device_id={"page": partner},
                device_id_type=MESH,
            ),
        )

    if lanes > 1:
        for copy in page_copies():
            copy.start()
    stat_row = lax.broadcasted_iota(jnp.int32, (16, 128), 0)
    empty = jnp.where(stat_row < kv, NEG, 0.0).astype(jnp.bfloat16)
    stat_at = pl.ds(kv * rows, 16)
    fresh_k[...] = jnp.zeros_like(fresh_k)
    fresh_v[...] = jnp.zeros_like(fresh_v)
    for n in range(steps):
        fresh_k[n * reqs : (n + 1) * reqs, :] = nk_ref[n]
        fresh_v[n * reqs : (n + 1) * reqs, :] = nv_ref[n]

    @pl.when(z == 0)
    def _():
        @pl.loop(0, nodes)
        def _(d):
            @pl.loop(0, reqs)
            def _(r):
                pin[d, r] = jnp.zeros((kv * rows + 16, HD), jnp.bfloat16)
                pin[d, r, pl.ds(kv * rows, 16), :] = empty

    @pl.when(zr == 0)
    def _():
        @pl.loop(0, nodes)
        def _(d):
            slot = jnp.where(d == nodes - 1, nodes, d)

            @pl.loop(0, reqs)
            def _(r):
                pin[slot, r] = jnp.zeros((kv * rows + 16, HD), jnp.bfloat16)
                pin[slot, r, pl.ds(kv * rows, 16), :] = empty

    def take_meta(page_at, k, heights, first):
        copies = []
        for n, height in enumerate(heights):
            got = mbuf.at[page_at, pl.ds(n * 8, height)]
            pltpu.make_async_copy(got, got, meta_recv.at[page_at, n]).wait()
            copies.append(
                pltpu.make_async_copy(
                    got, msm.at[page_at, pl.ds(first + n * 8, height)], meta_local.at[k, n]
                )
            )
        for copy in copies:
            copy.start()
        return copies

    def settle():
        taken = []
        for k in range(1, nodes):
            taken += take_meta(lax.rem(z + k, nodes) * lanes + lane, k, (levels, levels), 0)
        if lanes > 1:
            taken += take_meta(partner, nodes, (1,), 16)
        for copy in taken:
            copy.wait()
        for copy in local_copies:
            copy.wait()
        if lanes > 1:
            for copy in page_copies():
                copy.wait_recv()

    eye = lax.broadcasted_iota(jnp.int32, (rows, 128), 0) == lax.broadcasted_iota(
        jnp.int32, (rows, 128), 1
    )
    token = lax.broadcasted_iota(jnp.int32, (rows, tok), 1)

    def to_column(row):
        return jnp.sum(
            jnp.where(eye, jnp.broadcast_to(row, (rows, 128)), 0.0), axis=1, keepdims=True
        )

    def to_row(column):
        return jnp.sum(
            jnp.where(eye, jnp.broadcast_to(column, (rows, 128)), 0.0), axis=0, keepdims=True
        )

    def scores_of(query, keys):
        return (
            lax.dot_general(
                query, keys, (((1,), (1,)), ((), ())), preferred_element_type=jnp.float32
            )
            * scale
        )

    def page_of(node, r):
        found = []
        for o in range(lanes):
            owner = z * lanes + o
            slot = jnp.int32(0)
            hit = jnp.int32(0)
            for j in range(levels):
                match = msm[node * lanes + lane, j, r] == owner
                slot = jnp.where(match, msm[node * lanes + lane, 8 + j, r], slot)
                hit = jnp.where(match, 1, hit)
            found.append((slot, hit * msm[owner, 16, slot]))
        return found

    def page_scores(query, pages, h):
        cols = pl.ds(h * HD, HD)
        return [
            jnp.where(token < count, scores_of(query, kbuf[o, slot, :, cols]), NEG)
            for o, (slot, count) in enumerate(pages)
        ]

    def total_max(parts):
        wide = functools.reduce(jnp.maximum, [s for s in parts if s.shape[1] == tok])
        top = jnp.max(wide, axis=1, keepdims=True)
        for s in parts:
            if s.shape[1] != tok:
                top = jnp.maximum(top, jnp.max(s, axis=1, keepdims=True))
        return top

    def total_sum(parts):
        wide = functools.reduce(jnp.add, [w for w in parts if w.shape[1] == tok])
        total = jnp.sum(wide, axis=1, keepdims=True)
        for w in parts:
            if w.shape[1] != tok:
                total = total + jnp.sum(w, axis=1, keepdims=True)
        return total

    def attend(parts, values):
        heads = range(kv)
        tops = [total_max(parts[h]) for h in heads]
        weights = [[jnp.exp2(s - tops[h]) for s in parts[h]] for h in heads]
        accs = [
            functools.reduce(
                jnp.add,
                [
                    jnp.dot(w.astype(jnp.bfloat16), v, preferred_element_type=jnp.float32)
                    for w, v in zip(weights[h], values[h])
                ],
            )
            for h in heads
        ]
        return accs, tops, [total_sum(weights[h]) for h in heads]

    def stat_rows(packed):
        wide = packed.astype(jnp.float32)
        return [
            wide[h : h + 1] + (wide[kv + h : kv + h + 1] + wide[2 * kv + h : 2 * kv + h + 1])
            for h in range(kv)
        ]

    def pack_stats(columns):
        stat = jnp.zeros((16, 128), jnp.float32)
        for h, column in enumerate(columns):
            stat = jnp.where(lax.rem(stat_row, kv) == h, to_row(column), stat)
        first = stat.astype(jnp.bfloat16).astype(jnp.float32)
        rest = stat - first
        second = rest.astype(jnp.bfloat16).astype(jnp.float32)
        third = rest - second
        return jnp.where(
            stat_row < kv, first, jnp.where(stat_row < 2 * kv, second, third)
        ).astype(jnp.bfloat16)

    def span(h):
        return pl.ds(h * rows, rows)

    def partial(d, r):
        pages = page_of(d, r)
        parts = [page_scores(qbuf[d, r, span(h), :], pages, h) for h in range(kv)]
        values = [
            [vbuf[o, p[0], :, pl.ds(h * HD, HD)] for o, p in enumerate(pages)] for h in range(kv)
        ]
        accs, tops, totals = attend(parts, values)
        came = [to_column(row) for row in stat_rows(pin[d, r, stat_at, :])]
        outs, stats = [], []
        for h in range(kv):
            peak = jnp.maximum(tops[h], came[h])
            a = jnp.exp2(tops[h] - peak)
            b = jnp.exp2(came[h] - peak)
            mass = a * totals[h] + b
            inv = 1.0 / mass
            outs.append(
                accs[h] * (a * inv) + pin[d, r, span(h), :].astype(jnp.float32) * (b * inv)
            )
            stats.append(peak + jnp.log2(mass))
        for h in range(kv):
            pout[d, r, span(h), :] = outs[h].astype(jnp.bfloat16)
        pout[d, r, stat_at, :] = pack_stats(stats)

    new_pad = fresh_k.shape[0]
    new_token = lax.broadcasted_iota(jnp.int32, (rows, new_pad), 1)
    row_step = lax.broadcasted_iota(jnp.int32, (rows, new_pad), 0) // (rows // steps)
    causal = new_token // reqs <= row_step

    def local(r):
        pages = page_of(z, r)
        leaf_len = leaf_sm[0, r]
        fresh = causal & (lax.rem(new_token, reqs) == r)
        parts, values = [], []
        for h in range(kv):
            cols = pl.ds(h * HD, HD)
            query = q_ref[r, span(h), :]
            parts.append(
                page_scores(query, pages, h)
                + [
                    jnp.where(token < leaf_len, scores_of(query, lkbuf[r, :, cols]), NEG),
                    jnp.where(fresh, scores_of(query, fresh_k[:, cols]), NEG),
                ]
            )
            values.append(
                [vbuf[o, p[0], :, cols] for o, p in enumerate(pages)]
                + [lvbuf[r, :, cols], fresh_v[:, cols]]
            )
        accs, tops, totals = attend(parts, values)
        for h in range(kv):
            loc_o[r, span(h), :] = accs[h] * (1.0 / totals[h])
            loc_s[r, pl.ds(h, 1), :] = to_row(tops[h] + jnp.log2(totals[h]))

    def final(r):
        below_rows = stat_rows(pin[z, r, stat_at, :])
        above_rows = stat_rows(pin[nodes, r, stat_at, :])
        outs = []
        for h in range(kv):
            own = to_column(loc_s[r, pl.ds(h, 1), :])
            below = to_column(below_rows[h])
            above = to_column(above_rows[h])
            peak = jnp.maximum(own, jnp.maximum(below, above))
            a = jnp.exp2(own - peak)
            b = jnp.exp2(below - peak)
            c = jnp.exp2(above - peak)
            inv = 1.0 / (a + b + c)
            outs.append(
                loc_o[r, span(h), :] * (a * inv)
                + pin[z, r, span(h), :].astype(jnp.float32) * (b * inv)
                + pin[nodes, r, span(h), :].astype(jnp.float32) * (c * inv)
            )
        for h in range(kv):
            out_ref[r, span(h), :] = outs[h].astype(jnp.bfloat16)

    def chain_place(v, pos, delay):
        index = v - lag * pos - delay
        return index, lax.div(index, pieces), lax.rem(index, pieces)

    def early_of(pos):
        return jnp.minimum(lag * pos, pieces)

    def query_work(v, direction):
        pos = z if direction == 0 else zr
        index, s, i = chain_place(v, pos, 0)
        src_node = s if direction == 0 else nodes - 1 - s

        @pl.when((index >= 0) & (s < pos))
        def _():
            wait_q(src_node, i)

            @pl.when(pos < nodes - 1)
            def _():
                q_copy(direction, src_node, i, False).start()

        @pl.when((index >= 0) & (s == pos) & (i >= early_of(pos)) & (pos < nodes - 1))
        def _():
            q_copy(direction, z, i, True).start()

    def partial_work(v, direction):
        pos = z if direction == 0 else zr
        index, s, i = chain_place(v, pos, hold - early_of(pos))
        ahead = nodes + pos - s
        d = ahead if direction == 0 else nodes - 1 - ahead

        @pl.when((index >= 0) & (s > pos) & (s < nodes) & (pos < nodes - 1))
        def _():
            @pl.when(pos > 0)
            def _():
                wait_p(d, i)

            for j in range(rp):
                partial(d, i * rp + j)
            p_copy(direction, d, i).start()

    at_end = (z == 0) | (zr == 0)
    span_of_loop = max(
        [(nodes - 1) * pieces + lag * (nodes - 1), end_local + pieces, mid_local + pieces]
        + [nodes * pieces + lag * n + hold - min(lag * n, pieces) for n in range(nodes - 1)]
    )
    local_at = jnp.where(at_end, end_local, mid_local)
    settle_at = jnp.minimum(local_at, pieces + hold)

    for direction in range(2):
        pos = z if direction == 0 else zr

        @pl.when(pos < nodes - 1)
        def _():
            @pl.loop(0, early_of(pos))
            def _(i):
                q_copy(direction, z, i, True).start()

    @pl.loop(0, span_of_loop)
    def _(v):
        for direction in range(2):
            query_work(v, direction)

        @pl.when(v == settle_at)
        def _():
            settle()

        for direction in range(2):
            partial_work(v, direction)

        @pl.when((v >= local_at) & (v < local_at + pieces))
        def _():
            for j in range(rp):
                local((v - local_at) * rp + j)

    @pl.loop(0, pieces)
    def _(i):
        @pl.when(z > 0)
        def _():
            wait_p(z, i)

        @pl.when(zr > 0)
        def _():
            wait_p(nodes, i)

        for j in range(rp):
            final(i * rp + j)

    for k in range(1, meta_count + 1):
        for copy in meta_copies(k):
            copy.wait_send()
    if lanes > 1:
        for copy in page_copies():
            copy.wait_send()

    @pl.loop(0, pieces)
    def _(i):
        @pl.when(z + 1 < nodes)
        def _():
            q_copy(0, z, i, True).wait_send()

        @pl.when(z > 0)
        def _():
            q_copy(1, z, i, True).wait_send()

        @pl.loop(0, nodes)
        def _(n):
            @pl.when((n < z) & (z + 1 < nodes))
            def _():
                q_copy(0, n, i, False).wait_send()

            @pl.when((n > z) & (z > 0))
            def _():
                q_copy(1, n, i, False).wait_send()

            @pl.when(n > z)
            def _():
                p_copy(0, n, i).wait_send()

            @pl.when(n < z)
            def _():
                p_copy(1, n, i).wait_send()


def shards(
    queries,
    page_keys,
    page_values,
    page_count,
    leaf_keys,
    leaf_values,
    leaf_count,
    new_keys,
    new_values,
    path_owner,
    path_slot,
    lanes,
):
    reqs, steps, head_width = queries.shape
    pages, tok, kv_width = page_keys.shape
    kv = kv_width // HD
    group = QH // KVH
    rows = steps * group
    levels = path_owner.shape[1]
    owners = lax.axis_size("page")
    nodes = owners // lanes
    small = nodes <= 8
    rp = 1 if small else reqs
    pieces = reqs // rp
    lag = LAG if small else 1
    hold = max(0, lag * (nodes - 1) - pieces)
    mid_local = pieces
    end_local = END_LOCAL * pieces if small else nodes * pieces
    query_rows = (
        queries.reshape(reqs, steps, kv, group, HD)
        .transpose(0, 2, 1, 3, 4)
        .reshape(reqs, kv * rows, HD)
    )
    assert 3 * kv <= 16 and rows <= 128 and levels <= 8
    cfg = (lanes, nodes, reqs, kv, rows, steps, levels, tok, rp, lag, hold, end_local, mid_local)
    vmem = pl.BlockSpec(memory_space=pltpu.VMEM)
    hbm = pl.BlockSpec(memory_space=pl.ANY)
    dma = pltpu.SemaphoreType.DMA
    block = (reqs, kv * rows, HD)
    stat = (reqs, 8, 128)
    sent = (reqs, kv * rows + 16, HD)
    fresh_rows = -(-steps * reqs // 16) * 16
    out = pl.pallas_call(
        functools.partial(kernel, cfg),
        out_shape=jax.ShapeDtypeStruct(block, jnp.bfloat16),
        in_specs=[vmem, hbm, hbm, hbm, hbm, vmem, vmem, hbm, hbm, hbm, hbm],
        out_specs=vmem,
        scratch_shapes=[
            pltpu.VMEM((nodes,) + block, jnp.bfloat16),
            pltpu.VMEM((lanes,) + page_keys.shape, jnp.bfloat16),
            pltpu.VMEM((lanes,) + page_keys.shape, jnp.bfloat16),
            pltpu.VMEM(leaf_keys.shape, jnp.bfloat16),
            pltpu.VMEM(leaf_keys.shape, jnp.bfloat16),
            pltpu.VMEM((owners, 16, pages), jnp.int32),
            pltpu.SMEM((owners, 24, pages), jnp.int32),
            pltpu.SMEM((1, reqs), jnp.int32),
            pltpu.VMEM((fresh_rows, kv_width), jnp.bfloat16),
            pltpu.VMEM((fresh_rows, kv_width), jnp.bfloat16),
            pltpu.VMEM((nodes,) + sent, jnp.bfloat16),
            pltpu.VMEM((nodes + 1,) + sent, jnp.bfloat16),
            pltpu.VMEM(block, jnp.float32),
            pltpu.VMEM(stat, jnp.float32),
            dma((2, nodes, pieces)),
            dma((nodes, pieces)),
            dma((nodes, pieces)),
            dma((nodes + 1, pieces)),
            dma((2,)),
            dma((2,)),
            dma((2,)),
            dma((2,)),
            dma((nodes + 1, 2)),
            dma((owners, 2)),
            dma((nodes + 1, 4)),
        ],
        compiler_params=pltpu.CompilerParams(
            collective_id=0, has_side_effects=True, vmem_limit_bytes=60 * 1024 * 1024
        ),
    )(
        query_rows,
        page_keys,
        page_values,
        leaf_keys,
        leaf_values,
        new_keys.transpose(1, 0, 2),
        new_values.transpose(1, 0, 2),
        path_owner.T,
        path_slot.T,
        page_count[None, :],
        leaf_count[None, :],
    )
    return (
        out.reshape(reqs, kv, steps, group, HD)
        .transpose(0, 2, 1, 3, 4)
        .reshape(reqs, steps, head_width)
    )


LAG = 4
END_LOCAL = 3


def solution(mesh):
    lanes = 2 if mesh.shape["sub"] == 1 and mesh.shape["page"] % 4 == 0 else 1
    return jax.shard_map(
        functools.partial(shards, lanes=lanes),
        mesh=mesh,
        in_specs=(
            P(("groups", "page", "sub"), None, "head"),
            P(("groups", "page"), None, "head"),
            P(("groups", "page"), None, "head"),
            P(("groups", "page")),
            P(("groups", "page", "sub"), None, "head"),
            P(("groups", "page", "sub"), None, "head"),
            P(("groups", "page", "sub")),
            P(("groups", "page", "sub"), None, "head"),
            P(("groups", "page", "sub"), None, "head"),
            P(("groups", "page", "sub"), None),
            P(("groups", "page", "sub"), None),
        ),
        out_specs=P(("groups", "page", "sub"), None, "head"),
        check_vma=False,
    )
```
